128 devices in a mesh: ent: 8 (over y, core), grp: 16 (over x, z).
Axes of the slice: x: 4, y: 4, z: 4, core: 2. Of those that a mesh axis runs over, the one named last changes fastest.
Arguments:
- table: float32 [262144, 512], P(('ent', 'grp')), may hold values from -6 to 6
- touch_owner: int32 [65536, 1], P(('ent', 'grp')), may hold values from 0 to 127; in each aligned block of 512 rows (0 to 511, 512 to 1023, ...) at most 8 rows name the same one
- touch_local: int32 [65536], P(('ent', 'grp')), may hold values from 0 to 2047
- query_rel: int32 [32768], P(('ent', 'grp')), may hold values from 0 to 821
- neg_local: int32 [32768], P(('ent', 'grp')), may hold values from 0 to 2047
- rel_table: bfloat16 [822, 512], replicated, may hold values from -6 to 6
- in_gain: float32 [512], replicated, may hold values from 0.1 to 1.9
- out_gain: float32 [512], replicated, may hold values from 0.1 to 1.9
- w_gate: bfloat16 [512, 2048], replicated, may hold values from -0.25 to 0.25
- w_up: bfloat16 [512, 2048], replicated, may hold values from -0.25 to 0.25
- w_down: bfloat16 [2048, 512], replicated, may hold values from -0.125 to 0.125
Outputs:
- table_grad: float32 [262144, 512], P(('ent', 'grp'))
The draws below stay inside these ranges and needn't reach their ends.
Inputs may be any that keep to these rules, and one draw needn't show every extreme that they name: `touch_owner`: in each device's block of 512 references no owner is named more than 8 times, a bound that some block reaches.
All inputs are finite; a program needn't handle non-finite values.
Results may differ from the reference program's by a relative error of at most 0.0085.
Values may be sent and summed in bfloat16 or wider, within the bound.
A program may use at most 128 MiB of HBM per device.

```python
import math
import jax
import jax.numpy as jnp
import numpy as np
from jax import lax

D = 512
FF = 2048
NREL = 822
POS_WEIGHT = 64
NEG = 256
Q = 256
ROWS_DEV = 2048
CAP = 8
QUERIES = 32768
ROWS = 262144
N_ENT = 8
N_GRP = 16
DEVICES = 128


def plant(result, own_key, least, high):
    spot = [jax.random.randint(jax.random.fold_in(own_key, axis), (), 0, length) for axis, length in enumerate(result.shape)]
    widest = result.shape.index(max(result.shape))
    neighbour = spot[:widest] + [(spot[widest] + 1) % result.shape[widest]] + spot[widest + 1:]
    return result.at[tuple(spot)].set(least).at[tuple(neighbour)].set(high)


def level_of(key, shape, cuts, smallest, top_value):
    factor_of = 1.0
    for axis_at, blocks in cuts:
        heights = jax.random.uniform(jax.random.fold_in(jax.random.fold_in(key, 6), axis_at), (blocks,), jnp.float32, smallest / len(cuts), top_value / len(cuts))
        factor_of = factor_of * jnp.repeat(jnp.exp(heights), shape[axis_at] // blocks).reshape((-1,) + (1,) * (len(shape) - 1 - axis_at))
    return factor_of


def shared_out(rng, own, number, rows, number_of, top, most, skew):
    sequence = jax.random.permutation(rng, number_of)
    heavy_load, usual = load_shares(number_of, rows * top, most, skew, True), load_shares(number_of, rows * top, most, skew, False)
    places = jnp.arange(number_of)

    def named(tallies, turn):
        used = int((tallies > 0).sum())
        fixed = max(1, used // 4)
        moved = fixed + (places - fixed + turn * (used - fixed)) % max(1, number_of - fixed)
        return jnp.zeros((number_of,), jnp.int32).at[sequence[jnp.where(places < fixed, places, moved)]].set(jnp.asarray(tallies, jnp.int32))

    tallies = jnp.where(number % 4 == 0, named(heavy_load, number // 4), named(usual, number - number // 4 - 1))
    mixed = jax.random.permutation(jax.random.fold_in(own, 3), number_of)
    giver, sink = mixed[0:number_of // 2 * 2:2], mixed[1:number_of // 2 * 2:2]
    slack = jnp.minimum(tallies[giver] - 1, most - tallies[sink]) // 2
    slack = jnp.where((giver == sequence[0]) | (sink == sequence[0]) | (tallies[sink] == 0), 0, jnp.maximum(slack, 0))
    moved = jax.random.randint(jax.random.fold_in(own, 4), (number_of // 2,), 0, 1 << 20) % (slack + 1)
    tallies = tallies.at[giver].add(-moved).at[sink].add(moved)
    labels = jnp.searchsorted(jnp.cumsum(tallies), jnp.arange(rows * top), side="right").astype(jnp.int32)
    grid = labels.reshape(top, rows).T
    grid = grid[jax.random.permutation(jax.random.fold_in(own, 1), rows)]
    turn = jax.random.randint(jax.random.fold_in(own, 2), (rows, 1), 0, top)
    return jnp.take_along_axis(grid, (jnp.arange(top)[None, :] + turn) % top, axis=1)


def load_shares(count, total, most, slope, full):
    weights = [(1 << 20) // math.isqrt(standing ** slope) + 1 for standing in range(1, count + 1)]
    largest = most if full else min(most, max(-(-total // count), total * weights[0] // sum(weights)))
    least = 1 if total - largest >= count - 1 else 0
    counts, rest = [largest] + [least] * (count - 1), total - largest - least * (count - 1)
    while rest > 0:
        candidates = [i for i in range(1, count) if counts[i] < largest] or [i for i in range(1, count) if counts[i] < most]
        pool, remaining = sum([weights[i] for i in candidates]), rest
        for i in candidates:
            extra = min(most - counts[i], max(1, remaining * weights[i] // pool), rest)
            counts[i] = counts[i] + extra
            rest = rest - extra
    return np.array(counts)


def bell_draw(stream_key, dims, deviation, reach, cuts=(), kind=jnp.bfloat16):
    entries = deviation * jax.random.normal(stream_key, dims, jnp.float32)
    if cuts:
        entries = entries * level_of(stream_key, dims, cuts, -0.22, 0.18)
    return jnp.clip(entries, -reach, reach).astype(kind)


def setup_inputs(seed: int = 0) -> dict:
    key_list = jax.random.split(jax.random.key(seed), 12)
    table = bell_draw(key_list[0], (ROWS, D), 1.0, 6.0, ((0, 128),), jnp.float32)
    touch_owner_keys = jax.random.split(jax.random.fold_in(key_list[1], 1), (2 * QUERIES) // (2 * Q))
    touch_owner_turns = jax.random.permutation(jax.random.fold_in(key_list[1], 3), (2 * QUERIES) // (2 * Q))
    touch_owner = jax.vmap(lambda own, number: shared_out(jax.random.fold_in(key_list[1], 2), own, number, 2 * Q, DEVICES, 1, CAP, 2))(touch_owner_keys, touch_owner_turns).reshape((2 * QUERIES, 1))
    touch_local = plant(jax.random.randint(key_list[2], (2 * QUERIES,), 0, ROWS_DEV), jax.random.fold_in(key_list[2], 1), 0, ROWS_DEV - 1).astype(jnp.int32)
    query_rel = plant(jax.random.randint(key_list[3], (QUERIES,), 0, NREL), jax.random.fold_in(key_list[3], 1), 0, NREL - 1).astype(jnp.int32)
    neg_local = plant(jax.random.randint(key_list[4], (NEG * DEVICES,), 0, ROWS_DEV), jax.random.fold_in(key_list[4], 1), 0, ROWS_DEV - 1).astype(jnp.int32)
    rel_table = bell_draw(key_list[5], (NREL, D), 1.0, 6.0)
    in_gain = jnp.clip(1.0 + 0.18 * jax.random.normal(key_list[6], (D,), jnp.float32), 0.1, 1.9)
    out_gain = jnp.clip(1.0 + 0.18 * jax.random.normal(key_list[7], (D,), jnp.float32), 0.1, 1.9)
    w_gate = bell_draw(key_list[8], (D, FF), D ** -0.5, 0.25)
    w_up = bell_draw(key_list[9], (D, FF), D ** -0.5, 0.25)
    w_down = bell_draw(key_list[10], (FF, D), FF ** -0.5, 0.125)
    return dict(table=table, touch_owner=touch_owner, touch_local=touch_local, query_rel=query_rel, neg_local=neg_local, rel_table=rel_table, in_gain=in_gain, out_gain=out_gain, w_gate=w_gate, w_up=w_up, w_down=w_down)


norm_eps = 1e-06

def encode(head_rows, rel_rows, in_gain, out_gain, w_gate, w_up, w_down):
    base_sum = head_rows + rel_rows
    normed = (base_sum * lax.rsqrt(lax.optimization_barrier(jnp.mean(base_sum * base_sum, axis=-1, keepdims=True)) + norm_eps) * in_gain).astype(jnp.bfloat16)
    gate_proj = jnp.dot(normed, w_gate, preferred_element_type=jnp.float32)
    up_proj = jnp.dot(normed, w_up, preferred_element_type=jnp.float32)
    hidden = (jax.nn.silu(gate_proj) * up_proj).astype(jnp.bfloat16)
    mixed_sum = base_sum + jnp.dot(hidden, w_down, preferred_element_type=jnp.float32)
    return mixed_sum * lax.rsqrt(lax.optimization_barrier(jnp.mean(mixed_sum * mixed_sum, axis=-1, keepdims=True)) + norm_eps) * out_gain

def reference(table, touch_owner, touch_local, query_rel, neg_local, rel_table, in_gain, out_gain, w_gate, w_up, w_down):
    dev_count = N_ENT * N_GRP
    inv_scale = 1.0 / math.sqrt(D)
    row_ids = (touch_owner[:, 0].astype(jnp.int32) * ROWS_DEV + touch_local.astype(jnp.int32)).astype(jnp.int32)
    fetched = table[row_ids].astype(jnp.bfloat16).reshape(dev_count, 2, Q, D)
    head_rows = fetched[:, 0].reshape(N_ENT, N_GRP * Q, D)
    ctx_rows = fetched[:, 1].reshape(N_ENT, N_GRP * Q, D)
    rel_onehot = (query_rel[:, None] == jnp.arange(NREL, dtype=jnp.int32)[None, :]).astype(jnp.bfloat16)
    rel_rows = jnp.dot(rel_onehot, rel_table, preferred_element_type=jnp.float32).reshape(N_ENT, N_GRP * Q, D)
    neg_ids = (jnp.arange(dev_count, dtype=jnp.int32)[:, None] * ROWS_DEV + neg_local.astype(jnp.int32).reshape(dev_count, NEG)).astype(jnp.int32)
    negatives = table[neg_ids.reshape(-1)].astype(jnp.bfloat16).reshape(N_ENT, N_GRP * NEG, D)

    def per_group(operands):
        heads, contexts, relations, negs = operands

        def forward(head_f):
            return encode(head_f, relations, in_gain, out_gain, w_gate, w_up, w_down)
        query_vec, pullback = jax.vjp(forward, heads.astype(jnp.float32))
        query_bf = query_vec.astype(jnp.bfloat16)
        scores = jnp.dot(query_bf, negs.T, preferred_element_type=jnp.float32) * inv_scale
        neg_weight = (jax.nn.sigmoid(scores) * inv_scale).astype(jnp.bfloat16)
        ctx_f = contexts.astype(jnp.float32)
        pos_score = lax.optimization_barrier(jnp.sum(query_vec * ctx_f, axis=-1)) * inv_scale
        pos_weight = POS_WEIGHT * (jax.nn.sigmoid(pos_score) - 1.0) * inv_scale
        query_grad = jnp.dot(neg_weight, negs, preferred_element_type=jnp.float32) + pos_weight[:, None] * ctx_f
        ctx_grad = pos_weight[:, None] * query_vec
        head_grad = pullback(query_grad)[0]
        neg_grad = jnp.dot(neg_weight.T, query_bf, preferred_element_type=jnp.float32)
        return (head_grad, ctx_grad, neg_grad)
    head_grad, ctx_grad, neg_grad = lax.map(per_group, (head_rows, ctx_rows, rel_rows, negatives))
    ref_ids = row_ids.reshape(dev_count, 2, Q)
    table_grad = jnp.zeros((ROWS_DEV * dev_count, D), jnp.float32)
    table_grad = table_grad.at[ref_ids[:, 0].reshape(-1)].add(head_grad.reshape(-1, D))
    table_grad = table_grad.at[ref_ids[:, 1].reshape(-1)].add(ctx_grad.reshape(-1, D))
    table_grad = table_grad.at[neg_ids.reshape(-1)].add(neg_grad.reshape(-1, D))
    return table_grad
```

```python
import functools
import math

import jax
import jax.numpy as jnp
from jax import lax
from jax.experimental import pallas as pl
from jax.experimental.pallas import tpu as pltpu
from jax.sharding import PartitionSpec as P

MESH = pl.DeviceIdType.MESH
POS_WEIGHT = 64
EPS = 1e-06
BF = jnp.bfloat16
F32 = jnp.float32
I32 = jnp.int32
ENT = 8
GRP = 16
SIDE = 4
DEV = ENT * GRP
CAP = 8
SLOTS = DEV * CAP
REFS = 512
Q = 256
D = 512
FF = 2048
FC = 512
NFC = FF // FC
ROWS = 2048
NREL = 822
INV = 1.0 / math.sqrt(D)


def nn(a, b):
    return lax.dot_general(a, b, (((1,), (0,)), ((), ())), preferred_element_type=F32)


def nt(a, b):
    return lax.dot_general(a, b, (((1,), (1,)), ((), ())), preferred_element_type=F32)


def iota(shape, axis):
    return lax.broadcasted_iota(I32, shape, axis)


def hot(mask):
    return jnp.where(mask, 1.0, 0.0).astype(BF)


def column(row):
    return jnp.transpose(jnp.broadcast_to(row, (128, row.shape[1])))


class Gather:
    def __init__(self, ref, send, recv, me_e, me_g):
        self.ref, self.send, self.recv, self.me_e = ref, send, recv, me_e
        self.x, self.z = me_g // SIDE, me_g % SIDE
        self.copies = []

    def block(self, h, a1, a2):
        dx, dz = (a1, a2) if h == 0 else (a2, a1)
        return ((self.x + (dx + SIDE)) % SIDE) * SIDE + (self.z + (dz + SIDE)) % SIDE

    def slot(self, h, a1, a2, q):
        return (h * 16 + (a1 % SIDE) * SIDE + a2 % SIDE) * 2 + q

    def rows(self, h, a1, a2, part):
        lo, n = {None: (0, 128), 0: (0, 64), 1: (64, 64)}[part]
        return self.ref.at[self.block(h, a1, a2), pl.ds(h * 128 + lo, n), :]

    def push(self, h, a1, a2, part, t1, t2):
        r1, r2 = (a1 - t1) % SIDE, (a2 - t2) % SIDE
        i = len(self.copies)
        src = self.rows(h, a1, a2, part)
        copy = pltpu.make_async_remote_copy(
            src_ref=src,
            dst_ref=src,
            send_sem=self.send.at[i],
            recv_sem=self.recv.at[self.slot(h, r1, r2, part or 0)],
            device_id=(self.me_e, self.block(h, t1, t2)),
            device_id_type=MESH,
        )
        copy.start()
        self.copies.append(copy)

    def wait(self, h, a1, a2, part):
        view = self.rows(h, a1, a2, part)
        pltpu.make_async_copy(view, view, self.recv.at[self.slot(h, a1, a2, part or 0)]).wait()

    def second(self, h, a1):
        self.push(h, a1, 0, None, 0, 1)
        self.push(h, a1, 0, None, 0, -1)

    def stage0(self):
        for h in (0, 1):
            self.push(h, 0, 0, None, 1, 0)
            self.push(h, 0, 0, None, -1, 0)
        for h in (0, 1):
            self.second(h, 0)

    def stage1(self):
        for h in (0, 1):
            self.wait(h, -1, 0, None)
            self.push(h, -1, 0, 0, 1, 0)
            self.wait(h, 1, 0, None)
            self.push(h, 1, 0, 1, -1, 0)
        for h in (0, 1):
            self.second(h, -1)
            self.second(h, 1)
        self.across(0)

    def across(self, a1):
        for h in (0, 1):
            self.wait(h, a1, -1, None)
            self.push(h, a1, -1, 0, 0, 1)
            self.wait(h, a1, 1, None)
            self.push(h, a1, 1, 1, 0, -1)

    def stage2(self):
        for h in (0, 1):
            self.wait(h, 2, 0, 0)
            self.wait(h, 2, 0, 1)
            self.second(h, 2)

    def stage3(self):
        self.across(-1)
        self.across(1)
        self.across(2)

    def finish(self):
        for h in (0, 1):
            for a1 in (0, -1, 1, 2):
                self.wait(h, a1, 2, 0)
                self.wait(h, a1, 2, 1)

    def drain(self):
        for copy in self.copies:
            copy.wait_send()


def step_kernel(
    owner_ref, local_ref, rel_ref, neg_ref, gin_ref, gout_ref, tab_hbm, relt_hbm, wg_hbm, wu_hbm, wd_hbm,
    idrow_out, grads_out, negg_out,
    tab_f, tab_b, relt, wg, wu, wd,
    ids_s, ids_r, col_s, rows_s, rows_r, outg, back,
    negs, qall, base_s, gate_s, up_s, qvec_s, mix_s, acc_s, ctx_s,
    load_sem, a2a_send, a2a_recv, nsend, nrecv, qsend, qrecv,
):
    me_e, me_g = lax.axis_index("ent"), lax.axis_index("grp")
    me = me_e * GRP + me_g

    barrier = pltpu.get_barrier_semaphore()

    def greet(j, carry):
        t = (me + j) % DEV
        pl.semaphore_signal(barrier, inc=1, device_id=(t // GRP, t % GRP), device_id_type=MESH)
        return carry

    lax.fori_loop(1, DEV, greet, 0)

    loads = [
        pltpu.make_async_copy(src, dst, load_sem.at[i])
        for i, (src, dst) in enumerate(
            ((tab_hbm, tab_f), (relt_hbm, relt), (wg_hbm, wg), (wu_hbm, wu), (wd_hbm, wd))
        )
    ]
    for load in loads:
        load.start()

    def exchange(n, src, dst):
        def send(j, carry):
            t = (me + j) % DEV
            pltpu.make_async_remote_copy(
                src_ref=src.at[t],
                dst_ref=dst.at[me],
                send_sem=a2a_send.at[n],
                recv_sem=a2a_recv.at[n],
                device_id=(t // GRP, t % GRP),
                device_id_type=MESH,
            ).start()
            return carry

        lax.fori_loop(1, DEV, send, 0)
        dst[me] = src[me]

    def wait_all(buf, sem):
        view = buf.at[pl.ds(0, DEV - 1)]
        pltpu.make_async_copy(view, view, sem).wait()

    owner = owner_ref[...]
    local = local_ref[...]
    owner_t = hot(iota((DEV, REFS), 0) == owner)
    before = nn(owner_t, hot(iota((REFS, REFS), 0) < iota((REFS, REFS), 1)))
    placed = jnp.sum(before * owner_t.astype(F32), axis=0, keepdims=True).astype(I32)
    slot_row = owner * CAP + placed
    at = iota((128, REFS), 0) == placed
    high = (local // 256).astype(F32)
    low = (local % 256).astype(F32)
    zero = jnp.zeros((128, REFS), F32)
    ids = (
        256.0 * nt(owner_t, jnp.where(at, high, zero).astype(BF))
        + nt(owner_t, jnp.where(at, low, zero).astype(BF))
        + nt(owner_t, hot(at))
        - 1.0
    )
    ids_s[...] = ids.reshape(DEV, 1, 128)

    pl.semaphore_wait(barrier, DEV - 1)
    exchange(0, ids_s, ids_r)

    loads[0].wait()

    def narrow(i, carry):
        part = pl.ds(pl.multiple_of(i * 256, 256), 256)
        tab_b[part, :] = tab_f[part, :].astype(BF)
        return carry

    lax.fori_loop(0, ROWS // 256, narrow, 0)
    neg_col = column(neg_ref[...].astype(F32))[:, :1].astype(I32)
    negs[me_g] = nn(hot(neg_col == iota((Q, ROWS), 1)), tab_b[...]).astype(BF)
    ag_n = Gather(negs, nsend, nrecv, me_e, me_g)
    ag_n.stage0()

    wait_all(ids_r, a2a_recv.at[0])
    asked = ids_r[...].reshape(DEV, 128)
    asked_high = jnp.floor(asked * (1.0 / 256.0))
    asked_low = asked - 256.0 * asked_high
    spread = hot((iota((SLOTS, DEV), 0) // CAP) == iota((SLOTS, DEV), 1))
    mine = (iota((SLOTS, 128), 0) % CAP) == iota((SLOTS, 128), 1)
    slot_high = jnp.where(mine, nn(spread, asked_high.astype(BF)), 0.0)
    slot_low = jnp.where(mine, nn(spread, asked_low.astype(BF)), 0.0)
    ids_col = jnp.sum(256.0 * slot_high + slot_low, axis=1, keepdims=True)
    col_s[...] = jnp.broadcast_to(ids_col, (SLOTS, 128))
    ones = jnp.ones((8, 128), BF)
    idrow_out[...] = 256.0 * nt(ones, slot_high.astype(BF)) + nt(ones, slot_low.astype(BF))

    def look(i, carry):
        part = pl.ds(pl.multiple_of(i * 256, 256), 256)
        want = col_s[part, :][:, :1].astype(I32)
        found = nn(hot(want == iota((256, ROWS), 1)), tab_b[...])
        rows_s[pl.ds(i * 32, 32)] = found.reshape(32, CAP, D).astype(BF)
        return carry

    lax.fori_loop(0, SLOTS // 256, look, 0)
    exchange(1, rows_s, rows_r)
    ag_n.stage1()

    loads[1].wait()
    rel_col = column(rel_ref[...].astype(F32))[:, :1].astype(I32)
    rel_rows = nn(hot(rel_col == iota((Q, NREL), 1)), relt[...])
    slot_col = column(slot_row.astype(F32))[:, :1].astype(I32)
    pick = hot(slot_col == iota((REFS, SLOTS), 1))

    wait_all(rows_r, a2a_recv.at[1])
    came = rows_r[...].astype(F32).reshape(SLOTS, D).astype(BF)
    fetched = nn(pick, came)
    ctx_s[...] = fetched[Q:]
    base = fetched[:Q] + rel_rows
    base_s[...] = base
    r1 = lax.rsqrt(jnp.mean(base * base, axis=-1, keepdims=True) + EPS)
    normed = (base * r1 * gin_ref[...]).astype(BF)
    acc_s[...] = jnp.zeros((Q, D), F32)
    for load in loads[2:]:
        load.wait()

    def ahead(i, carry):
        part = pl.ds(pl.multiple_of(i * FC, FC), FC)
        g = nn(normed, wg[:, part])
        u = nn(normed, wu[:, part])
        gate_s[:, part] = g
        up_s[:, part] = u
        hidden = (g * jax.nn.sigmoid(g) * u).astype(BF)
        acc_s[...] += nn(hidden, wd[part, :])
        return carry

    lax.fori_loop(0, NFC, ahead, 0)
    mixed = base_s[...] + acc_s[...]
    r2 = lax.rsqrt(jnp.mean(mixed * mixed, axis=-1, keepdims=True) + EPS)
    query_vec = mixed * r2 * gout_ref[...]
    mix_s[...] = mixed
    qvec_s[...] = query_vec
    qall[me_g] = query_vec.astype(BF)
    ag_q = Gather(qall, qsend, qrecv, me_e, me_g)
    ag_q.stage0()
    ag_n.stage2()
    ag_n.stage3()
    ag_n.finish()

    def against(own, everyone):
        def body(i, carry):
            block = everyone[i]
            scores = nt(own, block) * (0.5 * INV)
            weight = ((0.5 * INV) * jnp.tanh(scores) + (0.5 * INV)).astype(BF)
            acc_s[...] += nn(weight, block)
            return carry

        acc_s[...] = jnp.zeros((Q, D), F32)
        lax.fori_loop(0, GRP, body, 0)

    against(qall[me_g], negs)
    ag_q.stage1()

    query_vec = qvec_s[...]
    ctx = ctx_s[...]
    pos_score = jnp.sum(query_vec * ctx, axis=-1, keepdims=True) * INV
    pos_weight = POS_WEIGHT * (jax.nn.sigmoid(pos_score) - 1.0) * INV
    query_grad = acc_s[...] + pos_weight * ctx
    ctx_grad = pos_weight * query_vec
    mixed = mix_s[...]
    r2 = lax.rsqrt(jnp.mean(mixed * mixed, axis=-1, keepdims=True) + EPS)
    t2 = query_grad * gout_ref[...]
    d_mixed = r2 * (t2 - mixed * (r2 * r2 * jnp.mean(t2 * mixed, axis=-1, keepdims=True)))
    d_mixed_b = d_mixed.astype(BF)
    acc_s[...] = jnp.zeros((Q, D), F32)

    def behind(i, carry):
        part = pl.ds(pl.multiple_of(i * FC, FC), FC)
        g = gate_s[:, part]
        u = up_s[:, part]
        s = jax.nn.sigmoid(g)
        dh = nt(d_mixed_b, wd[part, :]).astype(BF).astype(F32)
        du = (dh * (g * s)).astype(BF)
        dg = (dh * u * (s * (1.0 + g * (1.0 - s)))).astype(BF)
        acc_s[...] += nt(dg, wg[:, part]) + nt(du, wu[:, part])
        return carry

    lax.fori_loop(0, NFC, behind, 0)
    base = base_s[...]
    r1 = lax.rsqrt(jnp.mean(base * base, axis=-1, keepdims=True) + EPS)
    t1 = acc_s[...] * gin_ref[...]
    head_grad = d_mixed + r1 * (t1 - base * (r1 * r1 * jnp.mean(t1 * base, axis=-1, keepdims=True)))
    head_b = head_grad.astype(BF)
    ctx_b = ctx_grad.astype(BF)

    place = hot(iota((SLOTS, REFS), 0) == slot_row)
    out = nn(place[:, :Q], head_b) + nn(place[:, Q:], ctx_b)
    outg[...] = out.reshape(DEV, CAP, D).astype(BF)
    exchange(2, outg, back)
    ag_q.stage2()
    ag_q.stage3()
    ag_q.finish()

    against(negs[me_g], qall)
    total = acc_s[...]
    top = total.astype(BF)
    negg_out[:Q, :] = top
    negg_out[Q:, :] = (total - top.astype(F32)).astype(BF)

    wait_all(back, a2a_recv.at[2])
    grads_out[...] = back[...].astype(F32).reshape(SLOTS, D).astype(BF)
    wait_all(ids_s, a2a_send.at[0])
    wait_all(rows_s, a2a_send.at[1])
    wait_all(outg, a2a_send.at[2])
    ag_n.drain()
    ag_q.drain()


def place_kernel(idrow_ref, grads_ref, neg_ref, negg_ref, out_ref):
    first = pl.program_id(0) * 256
    slots = hot(iota((256, SLOTS), 0) + first == idrow_ref[...][:1, :].astype(I32))
    spans = hot(iota((256, Q), 0) + first == neg_ref[...])
    out_ref[...] = nn(slots, grads_ref[...]) + (nn(spans, negg_ref[:Q, :]) + nn(spans, negg_ref[Q:, :]))


def per_device(table, touch_owner, touch_local, query_rel, neg_local, rel_table, in_gain, out_gain, w_gate, w_up, w_down):
    neg_row = neg_local.reshape(1, Q)
    vmem = pl.BlockSpec(memory_space=pltpu.VMEM)
    hbm = pl.BlockSpec(memory_space=pl.ANY)
    idrow, grads, negg = pl.pallas_call(
        step_kernel,
        out_shape=(
            jax.ShapeDtypeStruct((8, SLOTS), F32),
            jax.ShapeDtypeStruct((SLOTS, D), BF),
            jax.ShapeDtypeStruct((2 * Q, D), BF),
        ),
        in_specs=[vmem] * 6 + [hbm] * 5,
        out_specs=(vmem, vmem, vmem),
        scratch_shapes=[
            pltpu.VMEM((ROWS, D), F32),
            pltpu.VMEM((ROWS, D), BF),
            pltpu.VMEM((NREL, D), BF),
            pltpu.VMEM((D, FF), BF),
            pltpu.VMEM((D, FF), BF),
            pltpu.VMEM((FF, D), BF),
            pltpu.VMEM((DEV, 1, 128), F32),
            pltpu.VMEM((DEV, 1, 128), F32),
            pltpu.VMEM((SLOTS, 128), F32),
            pltpu.VMEM((DEV, CAP, D), BF),
            pltpu.VMEM((DEV, CAP, D), BF),
            pltpu.VMEM((DEV, CAP, D), BF),
            pltpu.VMEM((DEV, CAP, D), BF),
            pltpu.VMEM((GRP, Q, D), BF),
            pltpu.VMEM((GRP, Q, D), BF),
            pltpu.VMEM((Q, D), F32),
            pltpu.VMEM((Q, FF), F32),
            pltpu.VMEM((Q, FF), F32),
            pltpu.VMEM((Q, D), F32),
            pltpu.VMEM((Q, D), F32),
            pltpu.VMEM((Q, D), F32),
            pltpu.VMEM((Q, D), F32),
            pltpu.SemaphoreType.DMA((5,)),
            pltpu.SemaphoreType.DMA((3,)),
            pltpu.SemaphoreType.DMA((3,)),
            pltpu.SemaphoreType.DMA((40,)),
            pltpu.SemaphoreType.DMA((64,)),
            pltpu.SemaphoreType.DMA((40,)),
            pltpu.SemaphoreType.DMA((64,)),
        ],
        compiler_params=pltpu.CompilerParams(
            collective_id=0, has_side_effects=True, vmem_limit_bytes=60 * 1024 * 1024
        ),
        name="step",
    )(
        touch_owner.reshape(1, REFS),
        touch_local.reshape(1, REFS),
        query_rel.reshape(1, Q),
        neg_row,
        in_gain.reshape(1, D),
        out_gain.reshape(1, D),
        table,
        rel_table,
        w_gate,
        w_up,
        w_down,
    )
    whole = lambda shape: pl.BlockSpec(shape, lambda i: (0, 0))
    return pl.pallas_call(
        place_kernel,
        grid=(ROWS // 256,),
        out_shape=jax.ShapeDtypeStruct((ROWS, D), F32),
        in_specs=[whole((8, SLOTS)), whole((SLOTS, D)), whole((1, Q)), whole((2 * Q, D))],
        out_specs=pl.BlockSpec((256, D), lambda i: (i, 0)),
        name="place",
    )(idrow, grads, neg_row, negg)


def solution(mesh):
    split = P(("ent", "grp"))
    rows = P(("ent", "grp"), None)
    return jax.shard_map(
        per_device,
        mesh=mesh,
        in_specs=(rows, rows, split, split, split, P(), P(), P(), P(), P(), P()),
        out_specs=rows,
        check_vma=False,
    )
```

```python
import functools
import math

import jax
import jax.numpy as jnp
from jax import lax
from jax.experimental import pallas as pl
from jax.experimental.pallas import tpu as pltpu
from jax.sharding import PartitionSpec as P

MESH = pl.DeviceIdType.MESH
POS_WEIGHT = 64
EPS = 1e-06
BF = jnp.bfloat16
F32 = jnp.float32
I32 = jnp.int32
ENT = 8
GRP = 16
SIDE = 4
DEV = ENT * GRP
CAP = 8
SLOTS = DEV * CAP
REFS = 512
Q = 256
D = 512
FF = 2048
FC = 512
NFC = FF // FC
ROWS = 2048
NREL = 822
TILE = 512
INV = 1.0 / math.sqrt(D)


def nn(a, b):
    return lax.dot_general(a, b, (((1,), (0,)), ((), ())), preferred_element_type=F32)


def nt(a, b):
    return lax.dot_general(a, b, (((1,), (1,)), ((), ())), preferred_element_type=F32)


def iota(shape, axis):
    return lax.broadcasted_iota(I32, shape, axis)


def hot(mask):
    return jnp.where(mask, 1.0, 0.0).astype(BF)


def column(row):
    return jnp.transpose(jnp.broadcast_to(row, (128, row.shape[1])))


class Gather:
    def __init__(self, ref, send, recv, me_e, me_g):
        self.ref, self.send, self.recv, self.me_e = ref, send, recv, me_e
        self.x, self.z = me_g // SIDE, me_g % SIDE
        self.copies = []

    def block(self, h, a1, a2):
        dx, dz = (a1, a2) if h == 0 else (a2, a1)
        return ((self.x + (dx + SIDE)) % SIDE) * SIDE + (self.z + (dz + SIDE)) % SIDE

    def slot(self, h, a1, a2, q):
        return (h * 16 + (a1 % SIDE) * SIDE + a2 % SIDE) * 2 + q

    def rows(self, h, a1, a2, part):
        lo, n = {None: (0, 128), 0: (0, 64), 1: (64, 64)}[part]
        return self.ref.at[self.block(h, a1, a2), pl.ds(h * 128 + lo, n), :]

    def push(self, h, a1, a2, part, t1, t2):
        r1, r2 = (a1 - t1) % SIDE, (a2 - t2) % SIDE
        i = len(self.copies)
        src = self.rows(h, a1, a2, part)
        copy = pltpu.make_async_remote_copy(
            src_ref=src,
            dst_ref=src,
            send_sem=self.send.at[i],
            recv_sem=self.recv.at[self.slot(h, r1, r2, part or 0)],
            device_id=(self.me_e, self.block(h, t1, t2)),
            device_id_type=MESH,
        )
        copy.start()
        self.copies.append(copy)

    def wait(self, h, a1, a2, part):
        view = self.rows(h, a1, a2, part)
        pltpu.make_async_copy(view, view, self.recv.at[self.slot(h, a1, a2, part or 0)]).wait()

    def second(self, h, a1):
        self.push(h, a1, 0, None, 0, 1)
        self.push(h, a1, 0, None, 0, -1)

    def stage0(self):
        for h in (0, 1):
            self.push(h, 0, 0, None, 1, 0)
            self.push(h, 0, 0, None, -1, 0)
        for h in (0, 1):
            self.second(h, 0)

    def stage1(self):
        for h in (0, 1):
            self.wait(h, -1, 0, None)
            self.push(h, -1, 0, 0, 1, 0)
            self.wait(h, 1, 0, None)
            self.push(h, 1, 0, 1, -1, 0)
        for h in (0, 1):
            self.second(h, -1)
            self.second(h, 1)

    def across(self, a1):
        for h in (0, 1):
            self.wait(h, a1, -1, None)
            self.push(h, a1, -1, 0, 0, 1)
            self.wait(h, a1, 1, None)
            self.push(h, a1, 1, 1, 0, -1)

    def stage2(self):
        for h in (0, 1):
            self.wait(h, 2, 0, 0)
            self.wait(h, 2, 0, 1)
            self.second(h, 2)

    def finish(self):
        for h in (0, 1):
            for a1 in (0, -1, 1, 2):
                self.wait(h, a1, 2, 0)
                self.wait(h, a1, 2, 1)

    def drain(self):
        for copy in self.copies:
            copy.wait_send()


def step_kernel(
    owner_ref, local_ref, rel_ref, neg_ref, gin_ref, gout_ref, tab_hbm, relt_hbm, wg_hbm, wu_hbm, wd_hbm,
    idrow_out, grads_out, negg_out,
    tab_f, tab_b, relt, wg, wu, wd,
    ids_s, ids_r, col_s, rows_s, rows_r, outg, back,
    negs, qring, part_s, part_r, sums, base_s, gate_s, up_s, qvec_s, mix_s, acc_s, ctx_s,
    load_sem, a2a_send, a2a_recv, nsend, nrecv, rsend, rrecv,
):
    me_e, me_g = lax.axis_index("ent"), lax.axis_index("grp")
    me = me_e * GRP + me_g

    barrier = pltpu.get_barrier_semaphore()

    others = [lax.rem(me_g + k, GRP) for k in range(GRP)]

    def each_peer(act, lo=0, hi=ENT):
        def across(j, carry):
            e = lax.rem(me_e + j, ENT)
            for g in others[1:]:
                act(e, g)
            return carry

        def along(j, carry):
            act(lax.rem(me_e + j, ENT), me_g)
            return carry

        lax.fori_loop(lo, hi, across, 0)
        lax.fori_loop(max(lo, 1), hi, along, 0)

    each_peer(
        lambda e, g: pl.semaphore_signal(barrier, inc=1, device_id=(e, g), device_id_type=MESH)
    )

    loads = [
        pltpu.make_async_copy(src, dst, load_sem.at[i])
        for i, (src, dst) in enumerate(
            ((tab_hbm, tab_f), (relt_hbm, relt), (wg_hbm, wg), (wu_hbm, wu), (wd_hbm, wd))
        )
    ]
    for load in loads:
        load.start()

    def exchange(n, src, dst, lo=0, hi=ENT):
        def send(e, g):
            pltpu.make_async_remote_copy(
                src_ref=src.at[e * GRP + g],
                dst_ref=dst.at[me],
                send_sem=a2a_send.at[n],
                recv_sem=a2a_recv.at[n],
                device_id=(e, g),
                device_id_type=MESH,
            ).start()

        each_peer(send, lo, hi)
        if lo == 0:
            dst[me] = src[me]

    def wait_all(buf, sem):
        view = buf.at[pl.ds(0, DEV - 1)]
        pltpu.make_async_copy(view, view, sem).wait()

    owner = owner_ref[...]
    local = local_ref[...]
    owner_t = hot(iota((DEV, REFS), 0) == owner)
    before = nn(owner_t, hot(iota((REFS, REFS), 0) < iota((REFS, REFS), 1)))
    placed = jnp.sum(before * owner_t.astype(F32), axis=0, keepdims=True).astype(I32)
    slot_row = owner * CAP + placed
    at = iota((128, REFS), 0) == placed
    high = (local // 256).astype(F32)
    low = (local % 256).astype(F32)
    zero = jnp.zeros((128, REFS), F32)
    ids = (
        256.0 * nt(owner_t, jnp.where(at, high, zero).astype(BF))
        + nt(owner_t, jnp.where(at, low, zero).astype(BF))
        + nt(owner_t, hot(at))
        - 1.0
    )
    ids_s[...] = ids.reshape(DEV, 1, 128)

    loads[0].wait()

    def narrow(i, carry):
        part = pl.ds(pl.multiple_of(i * 256, 256), 256)
        tab_b[part, :] = tab_f[part, :].astype(BF)
        return carry

    lax.fori_loop(0, ROWS // 256, narrow, 0)
    neg_col = column(neg_ref[...].astype(F32))[:, :1].astype(I32)
    negs[me_g] = nn(hot(neg_col == iota((Q, ROWS), 1)), tab_b[...]).astype(BF)
    ag_n = Gather(negs, nsend, nrecv, me_e, me_g)

    pl.semaphore_wait(barrier, DEV - 1)
    exchange(0, ids_s, ids_r)
    ag_n.stage0()

    wait_all(ids_r, a2a_recv.at[0])
    asked = ids_r[...].reshape(DEV, 128)
    asked_high = jnp.floor(asked * (1.0 / 256.0))
    asked_low = asked - 256.0 * asked_high
    spread = hot((iota((SLOTS, DEV), 0) // CAP) == iota((SLOTS, DEV), 1))
    mine = (iota((SLOTS, 128), 0) % CAP) == iota((SLOTS, 128), 1)
    slot_high = jnp.where(mine, nn(spread, asked_high.astype(BF)), 0.0)
    slot_low = jnp.where(mine, nn(spread, asked_low.astype(BF)), 0.0)
    ids_col = jnp.sum(256.0 * slot_high + slot_low, axis=1, keepdims=True)
    col_s[...] = jnp.broadcast_to(ids_col, (SLOTS, 128))
    ones = jnp.ones((8, 128), BF)
    idrow_out[...] = 256.0 * nt(ones, slot_high.astype(BF)) + nt(ones, slot_low.astype(BF))

    ag_n.stage1()

    def look(i, carry):
        part = pl.ds(pl.multiple_of(i * 256, 256), 256)
        want = col_s[part, :][:, :1].astype(I32)
        found = nn(hot(want == iota((256, ROWS), 1)), tab_b[...])
        rows_s[pl.ds(i * 32, 32)] = found.reshape(32, CAP, D).astype(BF)
        return carry

    lax.fori_loop(0, SLOTS // 256, look, 0)
    exchange(1, rows_s, rows_r)
    ag_n.across(0)
    ag_n.stage2()
    ag_n.across(-1)
    ag_n.across(1)

    loads[1].wait()
    rel_col = column(rel_ref[...].astype(F32))[:, :1].astype(I32)
    rel_rows = nn(hot(rel_col == iota((Q, NREL), 1)), relt[...])
    slot_col = column(slot_row.astype(F32))[:, :1].astype(I32)
    pick = hot(slot_col == iota((REFS, SLOTS), 1))

    wait_all(rows_r, a2a_recv.at[1])
    came = rows_r[...].astype(F32).reshape(SLOTS, D).astype(BF)
    fetched = nn(pick, came)
    ag_n.across(2)
    ctx_s[...] = fetched[Q:]
    base = fetched[:Q] + rel_rows
    base_s[...] = base
    r1 = lax.rsqrt(jnp.mean(base * base, axis=-1, keepdims=True) + EPS)
    normed = (base * r1 * gin_ref[...]).astype(BF)
    acc_s[...] = jnp.zeros((Q, D), F32)
    for load in loads[2:]:
        load.wait()

    def ahead(i, carry):
        part = pl.ds(pl.multiple_of(i * FC, FC), FC)
        g = nn(normed, wg[:, part])
        u = nn(normed, wu[:, part])
        gate_s[:, part] = g
        up_s[:, part] = u
        hidden = (g * jax.nn.sigmoid(g) * u).astype(BF)
        acc_s[...] += nn(hidden, wd[part, :])
        return carry

    lax.fori_loop(0, NFC, ahead, 0)
    mixed = base_s[...] + acc_s[...]
    r2 = lax.rsqrt(jnp.mean(mixed * mixed, axis=-1, keepdims=True) + EPS)
    query_vec = mixed * r2 * gout_ref[...]
    mix_s[...] = mixed
    qvec_s[...] = query_vec
    x, z = ag_n.x, ag_n.z
    query_b = query_vec.astype(BF)
    ring = []

    def hop(src, dst, sem, g):
        copy = pltpu.make_async_remote_copy(
            src_ref=src, dst_ref=dst, send_sem=rsend.at[sem], recv_sem=rrecv.at[sem],
            device_id=(me_e, g), device_id_type=MESH,
        )
        copy.start()
        ring.append(copy)

    def arrive(view, sem):
        pltpu.make_async_copy(view, view, rrecv.at[sem]).wait()

    ahead_of = lambda i, k: lax.rem(i + k, SIDE)
    rings = [
        (z, ahead_of(z, 1), ahead_of(z, 3), x * SIDE + ahead_of(z, 1), x * SIDE + ahead_of(z, 3)),
        (x, ahead_of(x, 1), ahead_of(x, 3), ahead_of(x, 1) * SIDE + z, ahead_of(x, 3) * SIDE + z),
    ]
    first, second = pl.ds(0, 128), pl.ds(128, 128)
    for k, (own, _, _, after, before_me) in enumerate(rings):
        qring[k, own] = query_b
        hop(qring.at[k, own], qring.at[k, own], 8 * k, after)
        hop(qring.at[k, own], qring.at[k, own], 8 * k + 1, before_me)

    def against(own, blocks):
        total = None
        for block in blocks:
            scores = nt(own, block) * (0.5 * INV)
            weight = ((0.5 * INV) * jnp.tanh(scores) + (0.5 * INV)).astype(BF)
            term = nn(weight, block)
            total = term if total is None else total + term
        return total

    def neg_at(dx, dz):
        return negs[lax.rem(x + (dx + SIDE), SIDE) * SIDE + lax.rem(z + (dz + SIDE), SIDE)]

    def near(i, carry):
        acc_s[...] += against(query_b, [neg_at(i - 1, dz) for dz in (-1, 0, 1)])
        return carry

    acc_s[...] = jnp.zeros((Q, D), F32)
    lax.fori_loop(0, 3, near, 0)
    ag_n.finish()
    acc_s[...] += against(query_b, [neg_at(dx, 2) for dx in (-1, 0, 1)])
    acc_s[...] += against(query_b, [neg_at(2, dz) for dz in (-1, 0, 1, 2)])

    query_vec = qvec_s[...]
    ctx = ctx_s[...]
    pos_score = jnp.sum(query_vec * ctx, axis=-1, keepdims=True) * INV
    pos_weight = POS_WEIGHT * (jax.nn.sigmoid(pos_score) - 1.0) * INV
    query_grad = acc_s[...] + pos_weight * ctx
    ctx_grad = pos_weight * query_vec
    mixed = mix_s[...]
    r2 = lax.rsqrt(jnp.mean(mixed * mixed, axis=-1, keepdims=True) + EPS)
    t2 = query_grad * gout_ref[...]
    d_mixed = r2 * (t2 - mixed * (r2 * r2 * jnp.mean(t2 * mixed, axis=-1, keepdims=True)))
    d_mixed_b = d_mixed.astype(BF)
    acc_s[...] = jnp.zeros((Q, D), F32)

    def behind(i, carry):
        part = pl.ds(pl.multiple_of(i * FC, FC), FC)
        g = gate_s[:, part]
        u = up_s[:, part]
        s = jax.nn.sigmoid(g)
        dh = nt(d_mixed_b, wd[part, :]).astype(BF).astype(F32)
        du = (dh * (g * s)).astype(BF)
        dg = (dh * u * (s * (1.0 + g * (1.0 - s)))).astype(BF)
        acc_s[...] += nt(dg, wg[:, part]) + nt(du, wu[:, part])
        return carry

    lax.fori_loop(0, NFC // 2, behind, 0)
    for k, (_, nxt, prev, after, before_me) in enumerate(rings):
        arrive(qring.at[k, prev], 8 * k)
        hop(qring.at[k, prev, first], qring.at[k, prev, first], 8 * k + 2, after)
        arrive(qring.at[k, nxt], 8 * k + 1)
        hop(qring.at[k, nxt, second], qring.at[k, nxt, second], 8 * k + 3, before_me)
    lax.fori_loop(NFC // 2, NFC, behind, 0)
    base = base_s[...]
    r1 = lax.rsqrt(jnp.mean(base * base, axis=-1, keepdims=True) + EPS)
    t1 = acc_s[...] * gin_ref[...]
    head_grad = d_mixed + r1 * (t1 - base * (r1 * r1 * jnp.mean(t1 * base, axis=-1, keepdims=True)))
    head_b = head_grad.astype(BF)
    ctx_b = ctx_grad.astype(BF)

    place = hot(iota((SLOTS, REFS), 0) == slot_row)
    out = nn(place[:, :Q], head_b) + nn(place[:, Q:], ctx_b)
    outg[...] = out.reshape(DEV, CAP, D).astype(BF)
    exchange(2, outg, back, 0, ENT // 2)

    upper, lower = pl.ds(0, 64), pl.ds(64, 64)
    for h in (0, 1):
        arrive(qring.at[h, 0, first], 8 * h + 2)
        arrive(qring.at[h, 0, second], 8 * h + 3)
        own = jnp.concatenate(
            [negs[ag_n.block(h, a, 0), h * 128 : h * 128 + 128] for a in (2, 1, -1, 0)], axis=0
        )
        terms = against(own, [qring[h, i] for i in range(SIDE)])
        part_s[h, 0] = terms[:128].astype(BF)
        sums[h] = terms[128:]
        _, _, _, after, before_me = rings[1 - h]
        hop(part_s.at[h, 0, upper], part_r.at[h, 0, upper], 8 * h + 4, after)
        hop(part_s.at[h, 0, lower], part_r.at[h, 0, lower], 8 * h + 5, before_me)
    exchange(2, outg, back, ENT // 2, ENT)
    for h in (0, 1):
        _, _, _, after, before_me = rings[1 - h]
        arrive(part_r.at[h, 0, upper], 8 * h + 4)
        part_s[h, 1, :64] = (sums[h, :64] + part_r[h, 0, :64].astype(F32)).astype(BF)
        part_s[h, 1, 64:] = sums[h, 64:128].astype(BF)
        hop(part_s.at[h, 1], part_r.at[h, 1], 8 * h + 6, after)
        arrive(part_r.at[h, 0, lower], 8 * h + 5)
        part_s[h, 2, :64] = sums[h, 128:192].astype(BF)
        part_s[h, 2, 64:] = (sums[h, 192:256] + part_r[h, 0, 64:].astype(F32)).astype(BF)
        hop(part_s.at[h, 2], part_r.at[h, 2], 8 * h + 7, before_me)
    for h in (0, 1):
        arrive(part_r.at[h, 1], 8 * h + 6)
        arrive(part_r.at[h, 2], 8 * h + 7)
        total = sums[h, 256:] + (part_r[h, 1].astype(F32) + part_r[h, 2].astype(F32))
        negg_out[h * 128 : h * 128 + 128, :] = total.astype(BF)

    wait_all(back, a2a_recv.at[2])
    grads_out[...] = back[...].astype(F32).reshape(SLOTS, D).astype(BF)
    wait_all(ids_s, a2a_send.at[0])
    wait_all(rows_s, a2a_send.at[1])
    wait_all(outg, a2a_send.at[2])
    ag_n.drain()
    for copy in ring:
        copy.wait_send()


def place_kernel(idrow_ref, grads_ref, neg_ref, negg_ref, out_ref):
    start = pl.program_id(0) * TILE
    slots = hot(iota((TILE, SLOTS), 0) + start == idrow_ref[...][:1, :].astype(I32))
    spans = hot(iota((TILE, Q), 0) + start == neg_ref[...])
    out_ref[...] = nn(slots, grads_ref[...]) + nn(spans, negg_ref[...])


def per_device(table, touch_owner, touch_local, query_rel, neg_local, rel_table, in_gain, out_gain, w_gate, w_up, w_down):
    neg_row = neg_local.reshape(1, Q)
    vmem = pl.BlockSpec(memory_space=pltpu.VMEM)
    hbm = pl.BlockSpec(memory_space=pl.ANY)
    idrow, grads, negg = pl.pallas_call(
        step_kernel,
        out_shape=(
            jax.ShapeDtypeStruct((8, SLOTS), F32),
            jax.ShapeDtypeStruct((SLOTS, D), BF),
            jax.ShapeDtypeStruct((Q, D), BF),
        ),
        in_specs=[vmem] * 6 + [hbm] * 5,
        out_specs=(vmem, vmem, vmem),
        scratch_shapes=[
            pltpu.VMEM((ROWS, D), F32),
            pltpu.VMEM((ROWS, D), BF),
            pltpu.VMEM((NREL, D), BF),
            pltpu.VMEM((D, FF), BF),
            pltpu.VMEM((D, FF), BF),
            pltpu.VMEM((FF, D), BF),
            pltpu.VMEM((DEV, 1, 128), F32),
            pltpu.VMEM((DEV, 1, 128), F32),
            pltpu.VMEM((SLOTS, 128), F32),
            pltpu.VMEM((DEV, CAP, D), BF),
            pltpu.VMEM((DEV, CAP, D), BF),
            pltpu.VMEM((DEV, CAP, D), BF),
            pltpu.VMEM((DEV, CAP, D), BF),
            pltpu.VMEM((GRP, Q, D), BF),
            pltpu.VMEM((2, SIDE, Q, D), BF),
            pltpu.VMEM((2, 3, 128, D), BF),
            pltpu.VMEM((2, 3, 128, D), BF),
            pltpu.VMEM((2, 384, D), F32),
            pltpu.VMEM((Q, D), F32),
            pltpu.VMEM((Q, FF), F32),
            pltpu.VMEM((Q, FF), F32),
            pltpu.VMEM((Q, D), F32),
            pltpu.VMEM((Q, D), F32),
            pltpu.VMEM((Q, D), F32),
            pltpu.VMEM((Q, D), F32),
            pltpu.SemaphoreType.DMA((5,)),
            pltpu.SemaphoreType.DMA((3,)),
            pltpu.SemaphoreType.DMA((3,)),
            pltpu.SemaphoreType.DMA((40,)),
            pltpu.SemaphoreType.DMA((64,)),
            pltpu.SemaphoreType.DMA((16,)),
            pltpu.SemaphoreType.DMA((16,)),
        ],
        compiler_params=pltpu.CompilerParams(
            collective_id=0, has_side_effects=True, vmem_limit_bytes=60 * 1024 * 1024
        ),
        name="step",
    )(
        touch_owner.reshape(1, REFS),
        touch_local.reshape(1, REFS),
        query_rel.reshape(1, Q),
        neg_row,
        in_gain.reshape(1, D),
        out_gain.reshape(1, D),
        table,
        rel_table,
        w_gate,
        w_up,
        w_down,
    )
    whole = lambda shape: pl.BlockSpec(shape, lambda i: (0, 0))
    return pl.pallas_call(
        place_kernel,
        grid=(ROWS // TILE,),
        out_shape=jax.ShapeDtypeStruct((ROWS, D), F32),
        in_specs=[whole((8, SLOTS)), whole((SLOTS, D)), whole((1, Q)), whole((Q, D))],
        out_specs=pl.BlockSpec((TILE, D), lambda i: (i, 0)),
        name="place",
    )(idrow, grads, neg_row, negg)


def solution(mesh):
    split = P(("ent", "grp"))
    rows = P(("ent", "grp"), None)
    return jax.shard_map(
        per_device,
        mesh=mesh,
        in_specs=(rows, rows, split, split, split, P(), P(), P(), P(), P(), P()),
        out_specs=rows,
        check_vma=False,
    )
```

```python
import functools
import math

import jax
import jax.numpy as jnp
from jax import lax
from jax.experimental import pallas as pl
from jax.experimental.pallas import tpu as pltpu
from jax.sharding import PartitionSpec as P

MESH = pl.DeviceIdType.MESH
POS_WEIGHT = 64
EPS = 1e-06
BF = jnp.bfloat16
F32 = jnp.float32
I32 = jnp.int32
ENT = 8
GRP = 16
SIDE = 4
DEV = ENT * GRP
CAP = 8
SLOTS = DEV * CAP
REFS = 512
Q = 256
D = 512
FF = 2048
FC = 512
NFC = FF // FC
ROWS = 2048
NREL = 822
TILE = 512
LOOK = 512
INV = 1.0 / math.sqrt(D)


def nn(a, b):
    return lax.dot_general(a, b, (((1,), (0,)), ((), ())), preferred_element_type=F32)


def nt(a, b):
    return lax.dot_general(a, b, (((1,), (1,)), ((), ())), preferred_element_type=F32)


def iota(shape, axis):
    return lax.broadcasted_iota(I32, shape, axis)


def hot(mask):
    return jnp.where(mask, 1.0, 0.0).astype(BF)


def column(row):
    return jnp.transpose(jnp.broadcast_to(row, (128, row.shape[1])))


class Gather:
    def __init__(self, ref, send, recv, me_e, me_g):
        self.ref, self.send, self.recv, self.me_e = ref, send, recv, me_e
        self.x, self.z = me_g // SIDE, me_g % SIDE
        self.copies = []

    def block(self, h, a1, a2):
        dx, dz = (a1, a2) if h == 0 else (a2, a1)
        return ((self.x + (dx + SIDE)) % SIDE) * SIDE + (self.z + (dz + SIDE)) % SIDE

    def slot(self, h, a1, a2, q):
        return (h * 16 + (a1 % SIDE) * SIDE + a2 % SIDE) * 2 + q

    def rows(self, h, a1, a2, part):
        lo, n = {None: (0, 128), 0: (0, 64), 1: (64, 64)}[part]
        return self.ref.at[self.block(h, a1, a2), pl.ds(h * 128 + lo, n), :]

    def push(self, h, a1, a2, part, t1, t2):
        r1, r2 = (a1 - t1) % SIDE, (a2 - t2) % SIDE
        i = len(self.copies)
        src = self.rows(h, a1, a2, part)
        copy = pltpu.make_async_remote_copy(
            src_ref=src,
            dst_ref=src,
            send_sem=self.send.at[i],
            recv_sem=self.recv.at[self.slot(h, r1, r2, part or 0)],
            device_id=(self.me_e, self.block(h, t1, t2)),
            device_id_type=MESH,
        )
        copy.start()
        self.copies.append(copy)

    def wait(self, h, a1, a2, part):
        view = self.rows(h, a1, a2, part)
        pltpu.make_async_copy(view, view, self.recv.at[self.slot(h, a1, a2, part or 0)]).wait()

    def second(self, h, a1):
        self.push(h, a1, 0, None, 0, 1)
        self.push(h, a1, 0, None, 0, -1)

    def stage0(self):
        for h in (0, 1):
            self.push(h, 0, 0, None, 1, 0)
            self.push(h, 0, 0, None, -1, 0)
        for h in (0, 1):
            self.second(h, 0)

    def stage1(self):
        for h in (0, 1):
            self.wait(h, -1, 0, None)
            self.push(h, -1, 0, 0, 1, 0)
            self.wait(h, 1, 0, None)
            self.push(h, 1, 0, 1, -1, 0)
        for h in (0, 1):
            self.second(h, -1)

    def across(self, a1):
        for h in (0, 1):
            self.wait(h, a1, -1, None)
            self.push(h, a1, -1, 0, 0, 1)
            self.wait(h, a1, 1, None)
            self.push(h, a1, 1, 1, 0, -1)

    def stage2(self):
        for h in (0, 1):
            self.wait(h, 2, 0, 0)
            self.wait(h, 2, 0, 1)
            self.second(h, 2)

    def finish(self):
        for h in (0, 1):
            for a1 in (0, -1, 1, 2):
                self.wait(h, a1, 2, 0)
                self.wait(h, a1, 2, 1)

    def drain(self):
        for copy in self.copies:
            copy.wait_send()


def step_kernel(
    owner_hbm, local_hbm, rel_hbm, neg_hbm, gin_hbm, gout_hbm, tab_hbm, relt_hbm, wg_hbm, wu_hbm, wd_hbm,
    idrow_out, back, negg_out,
    owner_ref, local_ref, rel_ref, neg_ref, gin_ref, gout_ref,
    tab_f, tab_b, relt, wg, wu, wd,
    ids_s, ids_r, col_s, idrow_s, rows_s, rows_r, outg,
    negs, qring, part_s, part_r, sums, base_s, gate_s, up_s, qvec_s, mix_s, acc_s, ctx_s,
    load_sem, a2a_send, a2a_recv, nsend, nrecv, rsend, rrecv,
):
    me_e, me_g = lax.axis_index("ent"), lax.axis_index("grp")
    me = me_e * GRP + me_g

    loads = [
        pltpu.make_async_copy(src, dst, load_sem.at[i])
        for i, (src, dst) in enumerate(
            (
                (owner_hbm, owner_ref), (local_hbm, local_ref), (neg_hbm, neg_ref), (rel_hbm, rel_ref),
                (gin_hbm, gin_ref), (gout_hbm, gout_ref),
                (tab_hbm, tab_f), (relt_hbm, relt), (wg_hbm, wg), (wu_hbm, wu), (wd_hbm, wd),
            )
        )
    ]
    for load in loads:
        load.start()

    barrier = pltpu.get_barrier_semaphore()

    span = lambda k: min(k, SIDE - k)
    away = sorted(range(1, GRP), key=lambda k: -(span(k // SIDE) + span(k % SIDE)))
    others = [
        lax.rem(me_g // SIDE + k // SIDE, SIDE) * SIDE + lax.rem(me_g % SIDE + k % SIDE, SIDE) for k in away
    ]

    def each_peer(act, lo=0, hi=ENT):
        def across(j, carry):
            e = lax.rem(me_e + (j + ENT // 2), ENT)
            for g in others:
                act(e, g)
            return carry

        def along(j, carry):
            act(lax.rem(me_e + (j + ENT // 2), ENT), me_g)
            return carry

        lax.fori_loop(lo, hi, across, 0)
        lax.fori_loop(lo, min(hi, ENT // 2), along, 0)
        lax.fori_loop(max(lo, ENT // 2 + 1), hi, along, 0)

    each_peer(
        lambda e, g: pl.semaphore_signal(barrier, inc=1, device_id=(e, g), device_id_type=MESH)
    )

    def exchange(n, src, dst, lo=0, hi=ENT):
        def send(e, g):
            pltpu.make_async_remote_copy(
                src_ref=src.at[e * GRP + g],
                dst_ref=dst.at[me],
                send_sem=a2a_send.at[n],
                recv_sem=a2a_recv.at[n],
                device_id=(e, g),
                device_id_type=MESH,
            ).start()

        each_peer(send, lo, hi)

    def wait_all(buf, sem):
        view = buf.at[pl.ds(0, DEV - 1)]
        pltpu.make_async_copy(view, view, sem).wait()

    for load in loads[:6]:
        load.wait()
    owner = owner_ref[...]
    local = local_ref[...]
    owner_t = hot(iota((DEV, REFS), 0) == owner)
    before = nn(owner_t, hot(iota((REFS, REFS), 0) < iota((REFS, REFS), 1)))
    placed = jnp.sum(before * owner_t.astype(F32), axis=0, keepdims=True).astype(I32)
    slot_row = owner * CAP + placed
    at = iota((128, REFS), 0) == placed
    high = (local // 256).astype(F32)
    low = (local % 256).astype(F32)
    zero = jnp.zeros((128, REFS), F32)
    ids = (
        256.0 * nt(owner_t, jnp.where(at, high, zero).astype(BF))
        + nt(owner_t, jnp.where(at, low, zero).astype(BF))
        + nt(owner_t, hot(at))
        - 1.0
    )
    ids_s[...] = ids.reshape(DEV, 1, 128)

    loads[6].wait()

    def narrow(i, carry):
        part = pl.ds(pl.multiple_of(i * 256, 256), 256)
        tab_b[part, :] = tab_f[part, :].astype(BF)
        return carry

    lax.fori_loop(0, ROWS // 256, narrow, 0)
    neg_col = column(neg_ref[...].astype(F32))[:, :1].astype(I32)
    negs[me_g] = nn(hot(neg_col == iota((Q, ROWS), 1)), tab_b[...]).astype(BF)
    ag_n = Gather(negs, nsend, nrecv, me_e, me_g)

    pl.semaphore_wait(barrier, DEV - 1)
    exchange(0, ids_s, ids_r)
    ids_r[me] = ids_s[me]
    ag_n.stage0()

    wait_all(ids_r, a2a_recv.at[0])
    asked = ids_r[...].reshape(DEV, 128)
    asked_high = jnp.floor(asked * (1.0 / 256.0))
    asked_low = asked - 256.0 * asked_high
    spread = hot((iota((SLOTS, DEV), 0) // CAP) == iota((SLOTS, DEV), 1))
    mine = (iota((SLOTS, 128), 0) % CAP) == iota((SLOTS, 128), 1)
    slot_high = jnp.where(mine, nn(spread, asked_high.astype(BF)), 0.0)
    slot_low = jnp.where(mine, nn(spread, asked_low.astype(BF)), 0.0)
    ids_col = jnp.sum(256.0 * slot_high + slot_low, axis=1, keepdims=True)
    col_s[...] = jnp.broadcast_to(ids_col, (SLOTS, 128))
    ones = jnp.ones((8, 128), BF)
    idrow_s[...] = 256.0 * nt(ones, slot_high.astype(BF)) + nt(ones, slot_low.astype(BF))

    ag_n.stage1()

    keep_ids = pltpu.make_async_copy(idrow_s, idrow_out, load_sem.at[0])
    keep_ids.start()

    def look(i, carry):
        part = pl.ds(pl.multiple_of(i * LOOK, LOOK), LOOK)
        want = col_s[part, :][:, :1].astype(I32)
        found = nn(hot(want == iota((LOOK, ROWS), 1)), tab_b[...])
        n = LOOK // CAP
        rows_s[pl.ds(i * n, n)] = found.reshape(n, CAP, D).astype(BF)
        return carry

    lax.fori_loop(0, SLOTS // LOOK, look, 0)
    exchange(1, rows_s, rows_r)
    rows_r[me] = rows_s[me]
    for h in (0, 1):
        ag_n.second(h, 1)
    ag_n.across(0)
    ag_n.stage2()
    ag_n.across(-1)

    loads[7].wait()
    rel_col = column(rel_ref[...].astype(F32))[:, :1].astype(I32)
    rel_rows = nn(hot(rel_col == iota((Q, NREL), 1)), relt[...])
    slot_col = column(slot_row.astype(F32))[:, :1].astype(I32)
    pick = hot(slot_col == iota((REFS, SLOTS), 1))

    wait_all(rows_r, a2a_recv.at[1])
    came = rows_r[...].astype(F32).reshape(SLOTS, D).astype(BF)
    fetched = nn(pick, came)
    ctx_s[...] = fetched[Q:]
    base = fetched[:Q] + rel_rows
    base_s[...] = base
    r1 = lax.rsqrt(jnp.mean(base * base, axis=-1, keepdims=True) + EPS)
    normed = (base * r1 * gin_ref[...]).astype(BF)
    acc_s[...] = jnp.zeros((Q, D), F32)
    for load in loads[8:]:
        load.wait()

    def ahead(i):
        part = slice(i * FC, i * FC + FC)
        g = nn(normed, wg[:, part])
        u = nn(normed, wu[:, part])
        s = jax.nn.sigmoid(g)
        silu = g * s
        up_s[:, part] = silu
        gate_s[:, part] = u * (s + silu * (1.0 - s))
        hidden = (silu * u).astype(BF)
        acc_s[...] += nn(hidden, wd[part, :])

    for i in range(NFC // 2):
        ahead(i)
    ag_n.across(1)
    for i in range(NFC // 2, NFC):
        ahead(i)
    mixed = base_s[...] + acc_s[...]
    r2 = lax.rsqrt(jnp.mean(mixed * mixed, axis=-1, keepdims=True) + EPS)
    query_vec = mixed * r2 * gout_ref[...]
    mix_s[...] = mixed
    qvec_s[...] = query_vec
    x, z = ag_n.x, ag_n.z
    query_b = query_vec.astype(BF)
    ring = []

    def hop(src, dst, sem, g):
        copy = pltpu.make_async_remote_copy(
            src_ref=src, dst_ref=dst, send_sem=rsend.at[sem], recv_sem=rrecv.at[sem],
            device_id=(me_e, g), device_id_type=MESH,
        )
        copy.start()
        ring.append(copy)

    def arrive(view, sem):
        pltpu.make_async_copy(view, view, rrecv.at[sem]).wait()

    odd = lax.rem(me_e, 2)
    even = 1 - odd
    here, line = z * even + x * odd, x * even + z * odd

    def along(k):
        i = lax.rem(here + k, SIDE)
        return i, (x * even + i * odd) * SIDE + (i * even + z * odd)

    def across(k):
        i = lax.rem(line + k, SIDE)
        return (i * even + x * odd) * SIDE + (z * even + i * odd)

    (nxt, after), (prev, ahead_me), (opposite, _) = along(1), along(3), along(2)
    first, second = pl.ds(0, 128), pl.ds(128, 128)

    def against(own, blocks):
        total = None
        for block in blocks:
            scores = nt(own, block) * (0.5 * INV)
            weight = ((0.5 * INV) * jnp.tanh(scores) + (0.5 * INV)).astype(BF)
            term = nn(weight, block)
            total = term if total is None else total + term
        return total

    def neg_at(dx, dz):
        return negs[lax.rem(x + (dx + SIDE), SIDE) * SIDE + lax.rem(z + (dz + SIDE), SIDE)]

    acc_s[...] = against(query_b, [neg_at(dx, dz) for dx in (-1, 0) for dz in (-1, 0, 1)])
    ag_n.across(2)
    qring[here] = query_b
    hop(qring.at[here], qring.at[here], 0, after)
    hop(qring.at[here], qring.at[here], 1, ahead_me)
    acc_s[...] += against(query_b, [neg_at(1, dz) for dz in (-1, 0, 1)])

    def lent(*ks):
        return jnp.concatenate([negs[across(k)] for k in ks], axis=0)

    sums[...] = against(lent(1, 3, 0), [query_b])
    ag_n.finish()
    arrive(qring.at[prev], 0)
    hop(qring.at[prev, first], qring.at[prev, first], 2, after)
    arrive(qring.at[nxt], 1)
    hop(qring.at[nxt, second], qring.at[nxt, second], 3, ahead_me)
    acc_s[...] += against(query_b, [neg_at(dx, 2) for dx in (-1, 0, 1)])
    acc_s[...] += against(query_b, [neg_at(2, dz) for dz in (-1, 0, 1, 2)])

    query_vec = qvec_s[...]
    ctx = ctx_s[...]
    pos_score = jnp.sum(query_vec * ctx, axis=-1, keepdims=True) * INV
    pos_weight = POS_WEIGHT * (jax.nn.sigmoid(pos_score) - 1.0) * INV
    query_grad = acc_s[...] + pos_weight * ctx
    ctx_grad = pos_weight * query_vec
    mixed = mix_s[...]
    r2 = lax.rsqrt(jnp.mean(mixed * mixed, axis=-1, keepdims=True) + EPS)
    t2 = query_grad * gout_ref[...]
    d_mixed = r2 * (t2 - mixed * (r2 * r2 * jnp.mean(t2 * mixed, axis=-1, keepdims=True)))
    d_mixed_b = d_mixed.astype(BF)
    acc_s[...] = jnp.zeros((Q, D), F32)

    def behind(i):
        part = slice(i * FC, i * FC + FC)
        dh = nt(d_mixed_b, wd[part, :]).astype(BF).astype(F32)
        du = (dh * up_s[:, part]).astype(BF)
        dg = (dh * gate_s[:, part]).astype(BF)
        acc_s[...] += nt(dg, wg[:, part]) + nt(du, wu[:, part])

    for i in range(NFC - 1):
        behind(i)
    arrive(qring.at[opposite, first], 2)
    arrive(qring.at[opposite, second], 3)
    part_s[0] = against(lent(2), [qring[i] for i in range(SIDE)]).astype(BF)
    hop(part_s.at[0, first], part_r.at[0, first], 4, across(1))
    hop(part_s.at[0, second], part_r.at[0, second], 5, across(3))
    behind(NFC - 1)
    base = base_s[...]
    r1 = lax.rsqrt(jnp.mean(base * base, axis=-1, keepdims=True) + EPS)
    t1 = acc_s[...] * gin_ref[...]
    head_grad = d_mixed + r1 * (t1 - base * (r1 * r1 * jnp.mean(t1 * base, axis=-1, keepdims=True)))
    head_b = head_grad.astype(BF)
    ctx_b = ctx_grad.astype(BF)

    place = hot(iota((SLOTS, REFS), 0) == slot_row)
    out = nn(place[:, :Q], head_b) + nn(place[:, Q:], ctx_b)
    outg[...] = out.reshape(DEV, CAP, D).astype(BF)
    exchange(2, outg, back)
    keep = pltpu.make_async_copy(outg.at[me], back.at[me], load_sem.at[1])
    keep.start()

    sums[...] += against(lent(1, 3, 0), [qring[prev], qring[nxt], qring[opposite]])
    arrive(part_r.at[0, first], 4)
    part_s[1, :128] = (sums[:128] + part_r[0, :128].astype(F32)).astype(BF)
    part_s[1, 128:] = sums[128:256].astype(BF)
    hop(part_s.at[1], part_r.at[1], 6, across(1))
    arrive(part_r.at[0, second], 5)
    part_s[2, :128] = sums[256:384].astype(BF)
    part_s[2, 128:] = (sums[384:512] + part_r[0, 128:].astype(F32)).astype(BF)
    hop(part_s.at[2], part_r.at[2], 7, across(3))
    arrive(part_r.at[1], 6)
    arrive(part_r.at[2], 7)
    negg_out[...] = (sums[512:] + (part_r[1].astype(F32) + part_r[2].astype(F32))).astype(BF)

    wait_all(back, a2a_recv.at[2])
    keep.wait()
    keep_ids.wait()
    wait_all(ids_s, a2a_send.at[0])
    wait_all(rows_s, a2a_send.at[1])
    wait_all(outg, a2a_send.at[2])
    ag_n.drain()
    for copy in ring:
        copy.wait_send()


def place_kernel(idrow_ref, back_ref, neg_ref, negg_ref, out_ref, grads):
    @pl.when(pl.program_id(0) == 0)
    def _():
        grads[...] = back_ref[...].astype(F32).reshape(SLOTS, D).astype(BF)

    start = pl.program_id(0) * TILE
    slots = hot(iota((TILE, SLOTS), 0) + start == idrow_ref[...][:1, :].astype(I32))
    spans = hot(iota((TILE, Q), 0) + start == neg_ref[...])
    out_ref[...] = nn(slots, grads[...]) + nn(spans, negg_ref[...])


def per_device(table, touch_owner, touch_local, query_rel, neg_local, rel_table, in_gain, out_gain, w_gate, w_up, w_down):
    neg_row = neg_local.reshape(1, Q)
    vmem = pl.BlockSpec(memory_space=pltpu.VMEM)
    hbm = pl.BlockSpec(memory_space=pl.ANY)
    idrow, grads, negg = pl.pallas_call(
        step_kernel,
        out_shape=(
            jax.ShapeDtypeStruct((8, SLOTS), F32),
            jax.ShapeDtypeStruct((DEV, CAP, D), BF),
            jax.ShapeDtypeStruct((Q, D), BF),
        ),
        in_specs=[hbm] * 11,
        out_specs=(hbm, hbm, vmem),
        scratch_shapes=[
            pltpu.VMEM((1, REFS), I32),
            pltpu.VMEM((1, REFS), I32),
            pltpu.VMEM((1, Q), I32),
            pltpu.VMEM((1, Q), I32),
            pltpu.VMEM((1, D), F32),
            pltpu.VMEM((1, D), F32),
            pltpu.VMEM((ROWS, D), F32),
            pltpu.VMEM((ROWS, D), BF),
            pltpu.VMEM((NREL, D), BF),
            pltpu.VMEM((D, FF), BF),
            pltpu.VMEM((D, FF), BF),
            pltpu.VMEM((FF, D), BF),
            pltpu.VMEM((DEV, 1, 128), F32),
            pltpu.VMEM((DEV, 1, 128), F32),
            pltpu.VMEM((SLOTS, 128), F32),
            pltpu.VMEM((8, SLOTS), F32),
            pltpu.VMEM((DEV, CAP, D), BF),
            pltpu.VMEM((DEV, CAP, D), BF),
            pltpu.VMEM((DEV, CAP, D), BF),
            pltpu.VMEM((GRP, Q, D), BF),
            pltpu.VMEM((SIDE, Q, D), BF),
            pltpu.VMEM((3, Q, D), BF),
            pltpu.VMEM((3, Q, D), BF),
            pltpu.VMEM((768, D), F32),
            pltpu.VMEM((Q, D), F32),
            pltpu.VMEM((Q, FF), F32),
            pltpu.VMEM((Q, FF), F32),
            pltpu.VMEM((Q, D), F32),
            pltpu.VMEM((Q, D), F32),
            pltpu.VMEM((Q, D), F32),
            pltpu.VMEM((Q, D), F32),
            pltpu.SemaphoreType.DMA((11,)),
            pltpu.SemaphoreType.DMA((3,)),
            pltpu.SemaphoreType.DMA((3,)),
            pltpu.SemaphoreType.DMA((40,)),
            pltpu.SemaphoreType.DMA((64,)),
            pltpu.SemaphoreType.DMA((8,)),
            pltpu.SemaphoreType.DMA((8,)),
        ],
        compiler_params=pltpu.CompilerParams(
            collective_id=0, has_side_effects=True, vmem_limit_bytes=60 * 1024 * 1024
        ),
        name="step",
    )(
        touch_owner.reshape(1, REFS),
        touch_local.reshape(1, REFS),
        query_rel.reshape(1, Q),
        neg_row,
        in_gain.reshape(1, D),
        out_gain.reshape(1, D),
        table,
        rel_table,
        w_gate,
        w_up,
        w_down,
    )
    whole = lambda shape: pl.BlockSpec(shape, lambda i: (0, 0))
    return pl.pallas_call(
        place_kernel,
        grid=(ROWS // TILE,),
        out_shape=jax.ShapeDtypeStruct((ROWS, D), F32),
        in_specs=[whole((8, SLOTS)), pl.BlockSpec((DEV, CAP, D), lambda i: (0, 0, 0)), whole((1, Q)), whole((Q, D))],
        out_specs=pl.BlockSpec((TILE, D), lambda i: (i, 0)),
        scratch_shapes=[pltpu.VMEM((SLOTS, D), BF)],
        name="place",
    )(idrow, grads, neg_row, negg)


def solution(mesh):
    split = P(("ent", "grp"))
    rows = P(("ent", "grp"), None)
    return jax.shard_map(
        per_device,
        mesh=mesh,
        in_specs=(rows, rows, split, split, split, P(), P(), P(), P(), P(), P()),
        out_specs=rows,
        check_vma=False,
    )
```

```python
import functools
import math

import jax
import jax.numpy as jnp
from jax import lax
from jax.experimental import pallas as pl
from jax.experimental.pallas import tpu as pltpu
from jax.sharding import PartitionSpec as P

MESH = pl.DeviceIdType.MESH
POS_WEIGHT = 64
EPS = 1e-06
BF = jnp.bfloat16
F32 = jnp.float32
I32 = jnp.int32
ENT = 8
GRP = 16
SIDE = 4
DEV = ENT * GRP
CAP = 8
SLOTS = DEV * CAP
REFS = 512
Q = 256
D = 512
FF = 2048
FC = 512
NFC = FF // FC
ROWS = 2048
NREL = 822
TILE = 1024
LOOK = 512
INV = 1.0 / math.sqrt(D)


def nn(a, b):
    return lax.dot_general(a, b, (((1,), (0,)), ((), ())), preferred_element_type=F32)


def nt(a, b):
    return lax.dot_general(a, b, (((1,), (1,)), ((), ())), preferred_element_type=F32)


def iota(shape, axis):
    return lax.broadcasted_iota(I32, shape, axis)


def hot(mask):
    return jnp.where(mask, 1.0, 0.0).astype(BF)


def column(row):
    return jnp.transpose(jnp.broadcast_to(row, (128, row.shape[1])))


class Gather:
    def __init__(self, ref, send, recv, me_e, me_g):
        self.ref, self.send, self.recv, self.me_e = ref, send, recv, me_e
        self.x, self.z = me_g // SIDE, me_g % SIDE
        self.copies = []

    def block(self, h, a1, a2):
        dx, dz = (a1, a2) if h == 0 else (a2, a1)
        return ((self.x + (dx + SIDE)) % SIDE) * SIDE + (self.z + (dz + SIDE)) % SIDE

    def slot(self, h, a1, a2, q):
        return (h * 16 + (a1 % SIDE) * SIDE + a2 % SIDE) * 2 + q

    def rows(self, h, a1, a2, part):
        lo, n = {None: (0, 128), 0: (0, 64), 1: (64, 64)}[part]
        return self.ref.at[self.block(h, a1, a2), pl.ds(h * 128 + lo, n), :]

    def push(self, h, a1, a2, part, t1, t2):
        r1, r2 = (a1 - t1) % SIDE, (a2 - t2) % SIDE
        i = len(self.copies)
        src = self.rows(h, a1, a2, part)
        copy = pltpu.make_async_remote_copy(
            src_ref=src,
            dst_ref=src,
            send_sem=self.send.at[i],
            recv_sem=self.recv.at[self.slot(h, r1, r2, part or 0)],
            device_id=(self.me_e, self.block(h, t1, t2)),
            device_id_type=MESH,
        )
        copy.start()
        self.copies.append(copy)

    def wait(self, h, a1, a2, part):
        view = self.rows(h, a1, a2, part)
        pltpu.make_async_copy(view, view, self.recv.at[self.slot(h, a1, a2, part or 0)]).wait()

    def second(self, h, a1):
        self.push(h, a1, 0, None, 0, 1)
        self.push(h, a1, 0, None, 0, -1)

    def stage0(self):
        for h in (0, 1):
            self.push(h, 0, 0, None, 1, 0)
            self.push(h, 0, 0, None, -1, 0)
        for h in (0, 1):
            self.second(h, 0)

    def stage1(self):
        for h in (0, 1):
            self.wait(h, -1, 0, None)
            self.push(h, -1, 0, 0, 1, 0)
            self.wait(h, 1, 0, None)
            self.push(h, 1, 0, 1, -1, 0)
        for h in (0, 1):
            self.second(h, -1)

    def across(self, a1):
        for h in (0, 1):
            self.wait(h, a1, -1, None)
            self.push(h, a1, -1, 0, 0, 1)
            self.wait(h, a1, 1, None)
            self.push(h, a1, 1, 1, 0, -1)

    def stage2(self):
        for h in (0, 1):
            self.wait(h, 2, 0, 0)
            self.wait(h, 2, 0, 1)
            self.second(h, 2)

    def finish(self):
        for h in (0, 1):
            for a1 in (0, -1, 1, 2):
                self.wait(h, a1, 2, 0)
                self.wait(h, a1, 2, 1)

    def drain(self):
        for copy in self.copies:
            copy.wait_send()


def step_kernel(
    owner_hbm, local_hbm, rel_hbm, neg_hbm, gin_hbm, gout_hbm, tab_hbm, relt_hbm, wg_hbm, wu_hbm, wd_hbm,
    idrow_out, back, negg_out,
    owner_ref, local_ref, rel_ref, neg_ref, gin_ref, gout_ref,
    tab_f, tab_b, relt, wg, wu, wd,
    ids_s, ids_r, col_s, idrow_s, rows_s, rows_r, outg,
    negs, qring, part_s, part_r, sums, base_s, gate_s, up_s, qvec_s, mix_s, acc_s, ctx_s,
    load_sem, a2a_send, a2a_recv, nsend, nrecv, rsend, rrecv,
):
    me_e, me_g = lax.axis_index("ent"), lax.axis_index("grp")
    me = me_e * GRP + me_g

    loads = [
        pltpu.make_async_copy(src, dst, load_sem.at[i])
        for i, (src, dst) in enumerate(
            (
                (owner_hbm, owner_ref), (local_hbm, local_ref), (neg_hbm, neg_ref), (rel_hbm, rel_ref),
                (gin_hbm, gin_ref), (gout_hbm, gout_ref),
                (tab_hbm, tab_f), (relt_hbm, relt), (wg_hbm, wg), (wu_hbm, wu), (wd_hbm, wd),
            )
        )
    ]
    for load in loads:
        load.start()

    barrier = pltpu.get_barrier_semaphore()

    span = lambda k: min(k, SIDE - k)
    away = sorted(range(1, GRP), key=lambda k: -(span(k // SIDE) + span(k % SIDE)))
    others = [
        lax.rem(me_g // SIDE + k // SIDE, SIDE) * SIDE + lax.rem(me_g % SIDE + k % SIDE, SIDE) for k in away
    ]

    def each_peer(act, lo=0, hi=ENT):
        def across(j, carry):
            e = lax.rem(me_e + (j + ENT // 2), ENT)
            for g in others:
                act(e, g)
            return carry

        def along(j, carry):
            act(lax.rem(me_e + (j + ENT // 2), ENT), me_g)
            return carry

        lax.fori_loop(lo, hi, across, 0)
        lax.fori_loop(lo, min(hi, ENT // 2), along, 0)
        lax.fori_loop(max(lo, ENT // 2 + 1), hi, along, 0)

    each_peer(
        lambda e, g: pl.semaphore_signal(barrier, inc=1, device_id=(e, g), device_id_type=MESH)
    )

    def exchange(n, src, dst, lo=0, hi=ENT):
        def send(e, g):
            pltpu.make_async_remote_copy(
                src_ref=src.at[e * GRP + g],
                dst_ref=dst.at[me],
                send_sem=a2a_send.at[n],
                recv_sem=a2a_recv.at[n],
                device_id=(e, g),
                device_id_type=MESH,
            ).start()

        each_peer(send, lo, hi)

    def wait_all(buf, sem):
        view = buf.at[pl.ds(0, DEV - 1)]
        pltpu.make_async_copy(view, view, sem).wait()

    for load in loads[:6]:
        load.wait()
    owner = owner_ref[...]
    local = local_ref[...]
    owner_t = hot(iota((DEV, REFS), 0) == owner)
    before = nn(owner_t, hot(iota((REFS, REFS), 0) < iota((REFS, REFS), 1)))
    placed = jnp.sum(before * owner_t.astype(F32), axis=0, keepdims=True).astype(I32)
    slot_row = owner * CAP + placed
    at = iota((128, REFS), 0) == placed
    high = (local // 256).astype(F32)
    low = (local % 256).astype(F32)
    zero = jnp.zeros((128, REFS), F32)
    ids = (
        256.0 * nt(owner_t, jnp.where(at, high, zero).astype(BF))
        + nt(owner_t, jnp.where(at, low, zero).astype(BF))
        + nt(owner_t, hot(at))
        - 1.0
    )
    ids_s[...] = ids.reshape(DEV, 1, 128)

    loads[6].wait()

    def narrow(i, carry):
        part = pl.ds(pl.multiple_of(i * 256, 256), 256)
        tab_b[part, :] = tab_f[part, :].astype(BF)
        return carry

    lax.fori_loop(0, ROWS // 256, narrow, 0)
    neg_col = column(neg_ref[...].astype(F32))[:, :1].astype(I32)
    negs[me_g] = nn(hot(neg_col == iota((Q, ROWS), 1)), tab_b[...]).astype(BF)
    ag_n = Gather(negs, nsend, nrecv, me_e, me_g)

    pl.semaphore_wait(barrier, DEV - 1)
    exchange(0, ids_s, ids_r)
    ids_r[me] = ids_s[me]
    ag_n.stage0()

    wait_all(ids_r, a2a_recv.at[0])
    asked = ids_r[...].reshape(DEV, 128)
    asked_high = jnp.floor(asked * (1.0 / 256.0))
    asked_low = asked - 256.0 * asked_high
    spread = hot((iota((SLOTS, DEV), 0) // CAP) == iota((SLOTS, DEV), 1))
    mine = (iota((SLOTS, 128), 0) % CAP) == iota((SLOTS, 128), 1)
    slot_high = jnp.where(mine, nn(spread, asked_high.astype(BF)), 0.0)
    slot_low = jnp.where(mine, nn(spread, asked_low.astype(BF)), 0.0)
    ids_col = jnp.sum(256.0 * slot_high + slot_low, axis=1, keepdims=True)
    col_s[...] = jnp.broadcast_to(ids_col, (SLOTS, 128))
    ones = jnp.ones((8, 128), BF)
    idrow_s[...] = 256.0 * nt(ones, slot_high.astype(BF)) + nt(ones, slot_low.astype(BF))

    ag_n.stage1()

    keep_ids = pltpu.make_async_copy(idrow_s, idrow_out, load_sem.at[0])
    keep_ids.start()

    def look(i, carry):
        part = pl.ds(pl.multiple_of(i * LOOK, LOOK), LOOK)
        want = col_s[part, :][:, :1].astype(I32)
        found = nn(hot(want == iota((LOOK, ROWS), 1)), tab_b[...])
        n = LOOK // CAP
        rows_s[pl.ds(i * n, n)] = found.reshape(n, CAP, D).astype(BF)
        return carry

    lax.fori_loop(0, SLOTS // LOOK, look, 0)
    exchange(1, rows_s, rows_r)
    rows_r[me] = rows_s[me]
    for h in (0, 1):
        ag_n.second(h, 1)
    ag_n.across(0)
    ag_n.stage2()
    ag_n.across(-1)

    loads[7].wait()
    rel_col = column(rel_ref[...].astype(F32))[:, :1].astype(I32)
    rel_rows = nn(hot(rel_col == iota((Q, NREL), 1)), relt[...])
    slot_col = column(slot_row.astype(F32))[:, :1].astype(I32)
    pick = hot(slot_col == iota((REFS, SLOTS), 1))

    wait_all(rows_r, a2a_recv.at[1])
    came = rows_r[...].astype(F32).reshape(SLOTS, D).astype(BF)
    fetched = nn(pick, came)
    ctx_s[...] = fetched[Q:]
    base = fetched[:Q] + rel_rows
    base_s[...] = base
    r1 = lax.rsqrt(jnp.mean(base * base, axis=-1, keepdims=True) + EPS)
    normed = (base * r1 * gin_ref[...]).astype(BF)
    acc_s[...] = jnp.zeros((Q, D), F32)
    for load in loads[8:]:
        load.wait()

    def ahead(i):
        part = slice(i * FC, i * FC + FC)
        g = nn(normed, wg[:, part])
        u = nn(normed, wu[:, part])
        s = jax.nn.sigmoid(g)
        silu = g * s
        up_s[:, part] = silu
        gate_s[:, part] = u * (s + silu * (1.0 - s))
        hidden = (silu * u).astype(BF)
        acc_s[...] += nn(hidden, wd[part, :])

    for i in range(NFC // 2):
        ahead(i)
    ag_n.across(1)
    for i in range(NFC // 2, NFC):
        ahead(i)
    mixed = base_s[...] + acc_s[...]
    r2 = lax.rsqrt(jnp.mean(mixed * mixed, axis=-1, keepdims=True) + EPS)
    query_vec = mixed * r2 * gout_ref[...]
    mix_s[...] = mixed
    qvec_s[...] = query_vec
    x, z = ag_n.x, ag_n.z
    query_b = query_vec.astype(BF)
    ring = []

    def hop(src, dst, sem, g):
        copy = pltpu.make_async_remote_copy(
            src_ref=src, dst_ref=dst, send_sem=rsend.at[sem], recv_sem=rrecv.at[sem],
            device_id=(me_e, g), device_id_type=MESH,
        )
        copy.start()
        ring.append(copy)

    def arrive(view, sem):
        pltpu.make_async_copy(view, view, rrecv.at[sem]).wait()

    odd = lax.rem(me_e, 2)
    even = 1 - odd
    here, line = z * even + x * odd, x * even + z * odd

    def along(k):
        i = lax.rem(here + k, SIDE)
        return i, (x * even + i * odd) * SIDE + (i * even + z * odd)

    def across(k):
        i = lax.rem(line + k, SIDE)
        return (i * even + x * odd) * SIDE + (z * even + i * odd)

    (nxt, after), (prev, ahead_me), (opposite, _) = along(1), along(3), along(2)
    first, second = pl.ds(0, 128), pl.ds(128, 128)

    def against(own, blocks):
        total = None
        for block in blocks:
            scores = nt(own, block) * (0.5 * INV)
            weight = ((0.5 * INV) * jnp.tanh(scores) + (0.5 * INV)).astype(BF)
            term = nn(weight, block)
            total = term if total is None else total + term
        return total

    def neg_at(dx, dz):
        return negs[lax.rem(x + (dx + SIDE), SIDE) * SIDE + lax.rem(z + (dz + SIDE), SIDE)]

    acc_s[...] = against(query_b, [neg_at(dx, dz) for dx in (-1, 0) for dz in (-1, 0, 1)])
    ag_n.across(2)
    qring[here] = query_b
    hop(qring.at[here], qring.at[here], 0, after)
    hop(qring.at[here], qring.at[here], 1, ahead_me)
    acc_s[...] += against(query_b, [neg_at(1, dz) for dz in (-1, 0, 1)])

    def lent(*ks):
        return jnp.concatenate([negs[across(k)] for k in ks], axis=0)

    sums[...] = against(lent(1, 3, 0), [query_b])
    ag_n.finish()
    acc_s[...] += against(query_b, [neg_at(dx, 2) for dx in (-1, 0, 1)])
    acc_s[...] += against(query_b, [neg_at(2, dz) for dz in (-1, 0, 1, 2)])

    arrive(qring.at[prev], 0)
    hop(qring.at[prev, first], qring.at[prev, first], 2, after)
    arrive(qring.at[nxt], 1)
    hop(qring.at[nxt, second], qring.at[nxt, second], 3, ahead_me)

    query_vec = qvec_s[...]
    ctx = ctx_s[...]
    pos_score = jnp.sum(query_vec * ctx, axis=-1, keepdims=True) * INV
    pos_weight = POS_WEIGHT * (jax.nn.sigmoid(pos_score) - 1.0) * INV
    query_grad = acc_s[...] + pos_weight * ctx
    ctx_grad = pos_weight * query_vec
    mixed = mix_s[...]
    r2 = lax.rsqrt(jnp.mean(mixed * mixed, axis=-1, keepdims=True) + EPS)
    t2 = query_grad * gout_ref[...]
    d_mixed = r2 * (t2 - mixed * (r2 * r2 * jnp.mean(t2 * mixed, axis=-1, keepdims=True)))
    d_mixed_b = d_mixed.astype(BF)
    acc_s[...] = jnp.zeros((Q, D), F32)

    def behind(i):
        part = slice(i * FC, i * FC + FC)
        dh = nt(d_mixed_b, wd[part, :]).astype(BF).astype(F32)
        du = (dh * up_s[:, part]).astype(BF)
        dg = (dh * gate_s[:, part]).astype(BF)
        acc_s[...] += nt(dg, wg[:, part]) + nt(du, wu[:, part])

    for i in range(NFC):
        behind(i)
    arrive(qring.at[opposite, first], 2)
    arrive(qring.at[opposite, second], 3)
    part_s[0] = against(lent(2), [qring[i] for i in range(SIDE)]).astype(BF)
    hop(part_s.at[0, first], part_r.at[0, first], 4, across(1))
    hop(part_s.at[0, second], part_r.at[0, second], 5, across(3))
    base = base_s[...]
    r1 = lax.rsqrt(jnp.mean(base * base, axis=-1, keepdims=True) + EPS)
    t1 = acc_s[...] * gin_ref[...]
    head_grad = d_mixed + r1 * (t1 - base * (r1 * r1 * jnp.mean(t1 * base, axis=-1, keepdims=True)))
    head_b = head_grad.astype(BF)
    ctx_b = ctx_grad.astype(BF)

    place = hot(iota((SLOTS, REFS), 0) == slot_row)
    out = nn(place[:, :Q], head_b) + nn(place[:, Q:], ctx_b)
    outg[...] = out.reshape(DEV, CAP, D).astype(BF)
    exchange(2, outg, back)
    keep = pltpu.make_async_copy(outg.at[me], back.at[me], load_sem.at[1])
    keep.start()

    sums[...] += against(lent(1, 3, 0), [qring[prev], qring[nxt], qring[opposite]])
    arrive(part_r.at[0, first], 4)
    part_s[1, :128] = (sums[:128] + part_r[0, :128].astype(F32)).astype(BF)
    part_s[1, 128:] = sums[128:256].astype(BF)
    hop(part_s.at[1], part_r.at[1], 6, across(1))
    arrive(part_r.at[0, second], 5)
    part_s[2, :128] = sums[256:384].astype(BF)
    part_s[2, 128:] = (sums[384:512] + part_r[0, 128:].astype(F32)).astype(BF)
    hop(part_s.at[2], part_r.at[2], 7, across(3))
    arrive(part_r.at[1], 6)
    arrive(part_r.at[2], 7)
    negg_out[...] = (sums[512:] + (part_r[1].astype(F32) + part_r[2].astype(F32))).astype(BF)

    wait_all(back, a2a_recv.at[2])
    keep.wait()
    keep_ids.wait()
    wait_all(ids_s, a2a_send.at[0])
    wait_all(rows_s, a2a_send.at[1])
    wait_all(outg, a2a_send.at[2])
    ag_n.drain()
    for copy in ring:
        copy.wait_send()


def place_kernel(idrow_ref, back_ref, neg_ref, negg_ref, out_ref, grads):
    @pl.when(pl.program_id(0) == 0)
    def _():
        grads[...] = back_ref[...].astype(F32).reshape(SLOTS, D).astype(BF)

    start = pl.program_id(0) * TILE
    slots = hot(iota((TILE, SLOTS), 0) + start == idrow_ref[...][:1, :].astype(I32))
    spans = hot(iota((TILE, Q), 0) + start == neg_ref[...])
    out_ref[...] = nn(slots, grads[...]) + nn(spans, negg_ref[...])


def per_device(table, touch_owner, touch_local, query_rel, neg_local, rel_table, in_gain, out_gain, w_gate, w_up, w_down):
    neg_row = neg_local.reshape(1, Q)
    vmem = pl.BlockSpec(memory_space=pltpu.VMEM)
    hbm = pl.BlockSpec(memory_space=pl.ANY)
    idrow, grads, negg = pl.pallas_call(
        step_kernel,
        out_shape=(
            jax.ShapeDtypeStruct((8, SLOTS), F32),
            jax.ShapeDtypeStruct((DEV, CAP, D), BF),
            jax.ShapeDtypeStruct((Q, D), BF),
        ),
        in_specs=[hbm] * 11,
        out_specs=(hbm, hbm, vmem),
        scratch_shapes=[
            pltpu.VMEM((1, REFS), I32),
            pltpu.VMEM((1, REFS), I32),
            pltpu.VMEM((1, Q), I32),
            pltpu.VMEM((1, Q), I32),
            pltpu.VMEM((1, D), F32),
            pltpu.VMEM((1, D), F32),
            pltpu.VMEM((ROWS, D), F32),
            pltpu.VMEM((ROWS, D), BF),
            pltpu.VMEM((NREL, D), BF),
            pltpu.VMEM((D, FF), BF),
            pltpu.VMEM((D, FF), BF),
            pltpu.VMEM((FF, D), BF),
            pltpu.VMEM((DEV, 1, 128), F32),
            pltpu.VMEM((DEV, 1, 128), F32),
            pltpu.VMEM((SLOTS, 128), F32),
            pltpu.VMEM((8, SLOTS), F32),
            pltpu.VMEM((DEV, CAP, D), BF),
            pltpu.VMEM((DEV, CAP, D), BF),
            pltpu.VMEM((DEV, CAP, D), BF),
            pltpu.VMEM((GRP, Q, D), BF),
            pltpu.VMEM((SIDE, Q, D), BF),
            pltpu.VMEM((3, Q, D), BF),
            pltpu.VMEM((3, Q, D), BF),
            pltpu.VMEM((768, D), F32),
            pltpu.VMEM((Q, D), F32),
            pltpu.VMEM((Q, FF), F32),
            pltpu.VMEM((Q, FF), F32),
            pltpu.VMEM((Q, D), F32),
            pltpu.VMEM((Q, D), F32),
            pltpu.VMEM((Q, D), F32),
            pltpu.VMEM((Q, D), F32),
            pltpu.SemaphoreType.DMA((11,)),
            pltpu.SemaphoreType.DMA((3,)),
            pltpu.SemaphoreType.DMA((3,)),
            pltpu.SemaphoreType.DMA((40,)),
            pltpu.SemaphoreType.DMA((64,)),
            pltpu.SemaphoreType.DMA((8,)),
            pltpu.SemaphoreType.DMA((8,)),
        ],
        compiler_params=pltpu.CompilerParams(
            collective_id=0, has_side_effects=True, vmem_limit_bytes=60 * 1024 * 1024
        ),
        name="step",
    )(
        touch_owner.reshape(1, REFS),
        touch_local.reshape(1, REFS),
        query_rel.reshape(1, Q),
        neg_row,
        in_gain.reshape(1, D),
        out_gain.reshape(1, D),
        table,
        rel_table,
        w_gate,
        w_up,
        w_down,
    )
    whole = lambda shape: pl.BlockSpec(shape, lambda i: (0, 0))
    return pl.pallas_call(
        place_kernel,
        grid=(ROWS // TILE,),
        out_shape=jax.ShapeDtypeStruct((ROWS, D), F32),
        in_specs=[whole((8, SLOTS)), pl.BlockSpec((DEV, CAP, D), lambda i: (0, 0, 0)), whole((1, Q)), whole((Q, D))],
        out_specs=pl.BlockSpec((TILE, D), lambda i: (i, 0)),
        scratch_shapes=[pltpu.VMEM((SLOTS, D), BF)],
        name="place",
    )(idrow, grads, neg_row, negg)


def solution(mesh):
    split = P(("ent", "grp"))
    rows = P(("ent", "grp"), None)
    return jax.shard_map(
        per_device,
        mesh=mesh,
        in_specs=(rows, rows, split, split, split, P(), P(), P(), P(), P(), P()),
        out_specs=rows,
        check_vma=False,
    )
```
